128 devices in a mesh: shard: 32 (over y, z, core), tensor: 2 (over x_lo), section: 2 (over x_hi).
Axes of the slice: x: 4 (x_hi: 2, x_lo: 2; x = x_hi * 2 + x_lo), y: 4, z: 4, core: 2. Of those that a mesh axis runs over, the one named last changes fastest.
Arguments:
- inputs: bfloat16 [131072, 1152], P(('shard', 'section')), may hold values from -12 to 12
- cotangent: bfloat16 [131072, 4608], P(('shard', 'section'), 'tensor'), may hold values from -0.015625 to 0.015625
- picks: int32 [1024], P(('shard', 'tensor', 'section')), may hold values from 0 to 2047
- master: float32 [2, 128, 144, 144], P('tensor', ('shard', 'section')), may hold values from -6 to 6
- velocity: float32 [2, 128, 144, 144], P('tensor', ('shard', 'section')), may hold values from -6 to 6
Outputs:
- velocity_next: float32 [2, 128, 144, 144], P('tensor', ('shard', 'section'))
- weights: bfloat16 [1152, 4608], P(None, 'tensor')
The draws below stay inside these ranges and needn't reach their ends.
All inputs are finite; a program needn't handle non-finite values. Where the reference program divides by a largest or mean magnitude, that divisor is 1e-20 or more.
Results may differ from the reference program's by a relative error of at most 0.001.
Values may be sent and summed in bfloat16 or wider, within the bound.
A program may use at most 192 MiB of HBM per device.

```python
import math
import jax
import jax.numpy as jnp
from jax import lax

D = 1152
H = 4608
BS = 144
ITERS = 4
SAMP = 8
TOK_DEV = 2048
TOKENS = 131072
TILES = 128
PICKS = 1024
N_SHARD = 32
N_TENSOR = 2
N_SECTION = 2


def draw_inputs(key, part):
    base_key, scale_key = jax.random.split(key, 2)
    columns = jnp.exp(jax.random.uniform(scale_key, (1, D), jnp.float32, math.log(0.5), math.log(2.0)))
    values = jnp.clip(jax.random.normal(base_key, (TOKENS, D), jnp.float32), -5.0, 5.0) * columns
    return jnp.clip(values, -12.0, 12.0).astype(jnp.bfloat16)


def touch_ends(entries, key, smallest, top_value):
    place = [jax.random.randint(jax.random.fold_in(key, axis), (), 0, length) for axis, length in enumerate(entries.shape)]
    main_axis = entries.shape.index(max(entries.shape))
    neighbour = place[:main_axis] + [(place[main_axis] + 1) % entries.shape[main_axis]] + place[main_axis + 1:]
    return entries.at[tuple(place)].set(smallest).at[tuple(neighbour)].set(top_value)


def levels(rng, shape, shards, least, high):
    loudness = 1.0
    for position, shards_of in shards:
        steps = jax.random.uniform(jax.random.fold_in(jax.random.fold_in(rng, 6), position), (shards_of,), jnp.float32, least / len(shards), high / len(shards))
        loudness = loudness * jnp.repeat(jnp.exp(steps), shape[position] // shards_of).reshape((-1,) + (1,) * (len(shape) - 1 - position))
    return loudness


def centred(rng, shape, width, most, cuts=(), kind=jnp.bfloat16):
    entries = jax.random.normal(rng, shape, jnp.float32) * width
    if len(cuts) > 0:
        entries = levels(rng, shape, cuts, -0.22, 0.18) * entries
    return jnp.clip(entries, min=-most, max=most).astype(kind)


def setup_inputs(seed: int = 0) -> dict:
    arg_keys = jax.random.split(jax.random.key(seed), 6)
    return {
        "inputs": draw_inputs(jax.random.fold_in(arg_keys[5], 71), 0),
        "cotangent": centred(arg_keys[1], (TOKENS, H), TOKENS ** -0.5, 0.015625, ((0, 64), (1, 2))),
        "picks": touch_ends(jax.random.randint(arg_keys[2], (PICKS,), 0, TOK_DEV), jax.random.fold_in(arg_keys[2], 1), 0, TOK_DEV - 1).astype(jnp.int32),
        "master": centred(arg_keys[3], (N_TENSOR, TILES, BS, BS), 1.0, 6.0, ((0, 2), (1, 64)), jnp.float32),
        "velocity": centred(arg_keys[4], (N_TENSOR, TILES, BS, BS), 0.5, 6.0, ((0, 2), (1, 64)), jnp.float32),
    }


damping = 0.1
momentum_rate = 0.9
learning_rate = 0.1


def invert_blocks(stats):
    order = stats.shape[-1]
    identity = jnp.eye(order, dtype=jnp.float32)
    damped = stats + damping * identity
    row_norm = jnp.max(jnp.sum(jnp.abs(damped), axis=2), axis=1)
    approx = identity[None] / row_norm[:, None, None]
    for sweep in range(ITERS):
        product = jnp.einsum("nij,njk->nik", damped, approx, precision=lax.Precision.HIGHEST)
        approx = 2.0 * approx - jnp.einsum("nij,njk->nik", approx, product, precision=lax.Precision.HIGHEST)
    return approx


def reference(inputs, cotangent, picks, master, velocity):
    row_blocks = D // BS
    half_width = H // N_TENSOR
    col_blocks = half_width // BS
    group_rows = (jnp.arange(N_SHARD, dtype=jnp.int32)[:, None] * N_SECTION
                  + jnp.arange(N_SECTION, dtype=jnp.int32)[None, :])
    layout = picks.reshape(N_SHARD, N_TENSOR, N_SECTION, SAMP).astype(jnp.int32)
    picked = (group_rows[:, None, :, None] * TOK_DEV + layout).astype(jnp.int32)
    samples = inputs[picked.reshape(-1)].astype(jnp.float32).reshape(-1, row_blocks, BS)
    input_stats = jnp.einsum("sir,sic->irc", samples, samples, precision=lax.Precision.HIGHEST) / PICKS
    output_list = []
    for tensor_rank in range(N_TENSOR):
        chosen = picked[:, tensor_rank].reshape(-1)
        grads = cotangent[chosen, tensor_rank * half_width:(tensor_rank + 1) * half_width]
        grads = grads.astype(jnp.float32).reshape(-1, col_blocks, BS)
        stats = jnp.einsum("sir,sic->irc", grads, grads, precision=lax.Precision.HIGHEST)
        output_list.append(stats * (TOKENS / (PICKS // N_TENSOR)))
    output_stats = jnp.stack(output_list)
    input_inverse = invert_blocks(input_stats)
    output_inverse = invert_blocks(output_stats.reshape(N_TENSOR * col_blocks, BS, BS)).reshape(N_TENSOR, col_blocks, BS, BS)

    def add_rows(shard_block, totals):
        start = (shard_block * TOK_DEV).astype(jnp.int32)
        left_rows = lax.dynamic_slice_in_dim(inputs, start, TOK_DEV, 0).astype(jnp.float32)
        right_rows = lax.dynamic_slice_in_dim(cotangent, start, TOK_DEV, 0).astype(jnp.float32)
        return totals + jnp.dot(left_rows.T, right_rows, precision=lax.Precision.HIGHEST)

    gradient = lax.fori_loop(0, N_SHARD * N_SECTION, add_rows, jnp.zeros((D, H), jnp.float32))
    tiles = gradient.reshape(row_blocks, BS, N_TENSOR, col_blocks, BS).transpose(2, 0, 3, 1, 4)
    left_side = jnp.einsum("irs,tijsc->tijrc", input_inverse, tiles, precision=lax.Precision.HIGHEST)
    update = jnp.einsum("tijrs,tjsc->tijrc", left_side, output_inverse, precision=lax.Precision.HIGHEST)
    update = update.reshape(N_TENSOR, TILES, BS, BS)
    velocity_next = momentum_rate * velocity + update
    fresh = (master - learning_rate * velocity_next).astype(jnp.bfloat16)
    weights = fresh.reshape(N_TENSOR, row_blocks, col_blocks, BS, BS).transpose(1, 3, 0, 2, 4).reshape(D, H)
    return velocity_next, weights
```

```python
import jax
import jax.numpy as jnp
from jax import lax
from jax.sharding import PartitionSpec as P

ITERS = 4
SAMP = 8


damping = 0.1
momentum_rate = 0.9
learning_rate = 0.1


def invert_blocks(stats):
    order = stats.shape[-1]
    identity = jnp.eye(order, dtype=jnp.float32)
    damped = stats + damping * identity
    row_norm = jnp.max(jnp.sum(jnp.abs(damped), axis=2), axis=1)
    approx = identity[None] / row_norm[:, None, None]
    for sweep in range(ITERS):
        product = jnp.einsum("nij,njk->nik", damped, approx, precision=lax.Precision.HIGHEST)
        approx = 2.0 * approx - jnp.einsum(
            "nij,njk->nik", approx, product, precision=lax.Precision.HIGHEST
        )
    return approx


def gram(rows):
    return jnp.einsum("sr,sc->rc", rows, rows, preferred_element_type=jnp.float32)


def body(inputs, cotangent, picks, master, velocity):
    token_rows, width = inputs.shape
    columns = cotangent.shape[1]
    block_size = master.shape[2]
    tiles_dev = master.shape[1]
    row_blocks = width // block_size
    col_blocks = columns // block_size
    count_input = SAMP * lax.axis_size("shard") * lax.axis_size("tensor") * lax.axis_size("section")
    count_output = SAMP * lax.axis_size("shard") * lax.axis_size("section")
    tokens_all = token_rows * lax.axis_size("shard") * lax.axis_size("section")

    first_tile = (
        lax.axis_index("shard") * lax.axis_size("section") + lax.axis_index("section")
    ) * tiles_dev
    positions = first_tile + jnp.arange(tiles_dev, dtype=jnp.int32)
    row_block = first_tile // col_blocks
    col_block_ids = positions % col_blocks

    sample_inputs = jnp.take(inputs, picks, axis=0)
    sample_grads = jnp.take(cotangent, picks, axis=0)
    all_inputs = lax.all_gather(sample_inputs, ("shard", "tensor", "section"), axis=0, tiled=True)
    all_grads = lax.all_gather(sample_grads, ("shard", "section"), axis=0, tiled=True)

    input_piece = lax.dynamic_slice_in_dim(all_inputs, row_block * block_size, block_size, 1)
    input_stats = gram(input_piece)[None] / count_input
    output_list = []
    for k in range(tiles_dev):
        piece = lax.dynamic_slice_in_dim(all_grads, col_block_ids[k] * block_size, block_size, 1)
        output_list.append(gram(piece) * (tokens_all / count_output))
    output_stats = jnp.stack(output_list)
    inverses = invert_blocks(jnp.concatenate([input_stats, output_stats], axis=0))
    left_inverse = inverses[0]
    right_inverse = inverses[1:]

    input_blocks = inputs.reshape(token_rows, row_blocks, block_size)
    grad_blocks = cotangent.reshape(token_rows, col_blocks, block_size)
    all_tiles = jnp.einsum(
        "tir,tjc->ijrc", input_blocks, grad_blocks, preferred_element_type=jnp.float32
    )
    all_tiles = all_tiles.reshape(row_blocks * col_blocks, block_size, block_size)
    summed = lax.psum(all_tiles, "section")
    owned_tiles = lax.psum_scatter(summed, "shard", scatter_dimension=0, tiled=True)
    grad_tiles = lax.dynamic_slice_in_dim(
        owned_tiles, lax.axis_index("section") * tiles_dev, tiles_dev, 0
    )
    left_side = jnp.einsum(
        "rs,ksc->krc", left_inverse, grad_tiles, precision=lax.Precision.HIGHEST
    )
    update = jnp.einsum("krs,ksc->krc", left_side, right_inverse, precision=lax.Precision.HIGHEST)
    velocity_next = momentum_rate * velocity + update[None]
    fresh = (master - learning_rate * velocity_next).astype(jnp.bfloat16)
    gathered = lax.all_gather(fresh, ("shard", "section"), axis=1, tiled=True)
    weights = (
        gathered.reshape(row_blocks, col_blocks, block_size, block_size)
        .transpose(0, 2, 1, 3)
        .reshape(width, columns)
    )
    return (velocity_next, weights)


def solution(mesh):
    placed = (
        P(("shard", "section"), None),
        P(("shard", "section"), "tensor"),
        P(("shard", "tensor", "section")),
        P("tensor", ("shard", "section"), None, None),
        P("tensor", ("shard", "section"), None, None),
    )
    return jax.shard_map(
        body,
        mesh=mesh,
        in_specs=placed,
        out_specs=(P("tensor", ("shard", "section"), None, None), P(None, "tensor")),
        check_vma=False,
    )
```

```python
import jax
import jax.numpy as jnp
from jax import lax
from jax.sharding import PartitionSpec as P

ITERS = 4
SAMP = 8


damping = 0.1
momentum_rate = 0.9
learning_rate = 0.1


def invert_blocks(stats):
    order = stats.shape[-1]
    identity = jnp.eye(order, dtype=jnp.float32)
    damped = stats + damping * identity
    row_norm = jnp.max(jnp.sum(jnp.abs(damped), axis=2), axis=1)
    approx = identity[None] / row_norm[:, None, None]
    for sweep in range(ITERS):
        product = jnp.einsum("nij,njk->nik", damped, approx, precision=lax.Precision.HIGHEST)
        approx = 2.0 * approx - jnp.einsum(
            "nij,njk->nik", approx, product, precision=lax.Precision.HIGHEST
        )
    return approx


def gram(rows):
    return jnp.einsum("sr,sc->rc", rows, rows, preferred_element_type=jnp.float32)


def body(inputs, cotangent, picks, master, velocity):
    token_rows, width = inputs.shape
    columns = cotangent.shape[1]
    block_size = master.shape[2]
    tiles_dev = master.shape[1]
    row_blocks = width // block_size
    col_blocks = columns // block_size
    count_input = SAMP * lax.axis_size("shard") * lax.axis_size("tensor") * lax.axis_size("section")
    count_output = SAMP * lax.axis_size("shard") * lax.axis_size("section")
    tokens_all = token_rows * lax.axis_size("shard") * lax.axis_size("section")

    first_tile = (
        lax.axis_index("shard") * lax.axis_size("section") + lax.axis_index("section")
    ) * tiles_dev
    positions = first_tile + jnp.arange(tiles_dev, dtype=jnp.int32)
    row_block = first_tile // col_blocks
    col_block_ids = positions % col_blocks

    section_index = lax.axis_index("section")
    swap = [(0, 1), (1, 0)]
    sample_rows = jnp.concatenate(
        [jnp.take(inputs, picks, axis=0), jnp.take(cotangent, picks, axis=0)], axis=1
    )
    rows_all = lax.all_gather(sample_rows, "shard", axis=0, tiled=True)
    input_piece = lax.dynamic_slice_in_dim(rows_all, row_block * block_size, block_size, 1)
    input_part = gram(input_piece)
    ring_first = (first_tile - section_index * tiles_dev) % col_blocks
    ring_parts = []
    for k in range(lax.axis_size("section") * tiles_dev):
        start = width + (ring_first + k) * block_size
        piece = lax.dynamic_slice_in_dim(rows_all, start, block_size, 1)
        ring_parts.append(gram(piece))
    ring_parts = jnp.stack(ring_parts)
    own_parts = lax.dynamic_slice_in_dim(ring_parts, section_index * tiles_dev, tiles_dev, 0)
    other_parts = lax.dynamic_slice_in_dim(
        ring_parts, (1 - section_index) * tiles_dev, tiles_dev, 0
    )
    sent = jnp.concatenate([input_part[None], other_parts], axis=0)
    got = lax.ppermute(sent, "section", swap)
    input_pair = input_part + got[0]
    input_sum = input_pair + lax.ppermute(input_pair, "tensor", swap)
    output_sum = own_parts + got[1:]
    input_stats = input_sum[None] / count_input
    output_stats = output_sum * (tokens_all / count_output)
    inverses = invert_blocks(jnp.concatenate([input_stats, output_stats], axis=0))
    left_inverse = inverses[0]
    right_inverse = inverses[1:]

    input_blocks = inputs.reshape(token_rows, row_blocks, block_size)
    grad_blocks = cotangent.reshape(token_rows, col_blocks, block_size)
    all_tiles = jnp.einsum(
        "tir,tjc->ijrc", input_blocks, grad_blocks, preferred_element_type=jnp.float32
    )
    all_tiles = all_tiles.reshape(row_blocks * col_blocks, block_size, block_size)
    owned_tiles = lax.psum_scatter(all_tiles, "shard", scatter_dimension=0, tiled=True)
    mine = lax.dynamic_slice_in_dim(owned_tiles, section_index * tiles_dev, tiles_dev, 0)
    theirs = lax.dynamic_slice_in_dim(owned_tiles, (1 - section_index) * tiles_dev, tiles_dev, 0)
    grad_tiles = mine + lax.ppermute(theirs, "section", swap)
    left_side = jnp.einsum(
        "rs,ksc->krc", left_inverse, grad_tiles, precision=lax.Precision.HIGHEST
    )
    update = jnp.einsum("krs,ksc->krc", left_side, right_inverse, precision=lax.Precision.HIGHEST)
    velocity_next = momentum_rate * velocity + update[None]
    fresh = (master - learning_rate * velocity_next).astype(jnp.bfloat16)
    gathered = lax.all_gather(fresh, ("shard", "section"), axis=1, tiled=True)
    weights = (
        gathered.reshape(row_blocks, col_blocks, block_size, block_size)
        .transpose(0, 2, 1, 3)
        .reshape(width, columns)
    )
    return (velocity_next, weights)


def solution(mesh):
    placed = (
        P(("shard", "section"), None),
        P(("shard", "section"), "tensor"),
        P(("shard", "tensor", "section")),
        P("tensor", ("shard", "section"), None, None),
        P("tensor", ("shard", "section"), None, None),
    )
    return jax.shard_map(
        body,
        mesh=mesh,
        in_specs=placed,
        out_specs=(P("tensor", ("shard", "section"), None, None), P(None, "tensor")),
        check_vma=False,
    )
```

```python
import jax
import jax.numpy as jnp
from jax import lax
from jax.sharding import PartitionSpec as P

ITERS = 4
SAMP = 8


damping = 0.1
momentum_rate = 0.9
learning_rate = 0.1


def invert_blocks(stats):
    order = stats.shape[-1]
    identity = jnp.eye(order, dtype=jnp.float32)
    damped = stats + damping * identity
    row_norm = jnp.max(jnp.sum(jnp.abs(damped), axis=2), axis=1)
    approx = identity[None] / row_norm[:, None, None]
    for sweep in range(ITERS):
        product = jnp.einsum("nij,njk->nik", damped, approx, precision=lax.Precision.HIGHEST)
        approx = 2.0 * approx - jnp.einsum(
            "nij,njk->nik", approx, product, precision=lax.Precision.HIGHEST
        )
    return approx


def gram(rows):
    return jnp.einsum("sr,sc->rc", rows, rows, preferred_element_type=jnp.float32)


def body(inputs, cotangent, picks, master, velocity):
    token_rows, width = inputs.shape
    columns = cotangent.shape[1]
    block_size = master.shape[2]
    tiles_dev = master.shape[1]
    row_blocks = width // block_size
    col_blocks = columns // block_size
    count_input = SAMP * lax.axis_size("shard") * lax.axis_size("tensor") * lax.axis_size("section")
    count_output = SAMP * lax.axis_size("shard") * lax.axis_size("section")
    tokens_all = token_rows * lax.axis_size("shard") * lax.axis_size("section")

    first_tile = (
        lax.axis_index("shard") * lax.axis_size("section") + lax.axis_index("section")
    ) * tiles_dev
    positions = first_tile + jnp.arange(tiles_dev, dtype=jnp.int32)
    row_block = first_tile // col_blocks
    col_block_ids = positions % col_blocks

    section_index = lax.axis_index("section")
    swap = [(0, 1), (1, 0)]
    sample_rows = jnp.concatenate(
        [jnp.take(inputs, picks, axis=0), jnp.take(cotangent, picks, axis=0)], axis=1
    )
    rows_all = lax.all_gather(sample_rows, "shard", axis=0, tiled=True)
    input_piece = lax.dynamic_slice_in_dim(rows_all, row_block * block_size, block_size, 1)
    input_part = gram(input_piece)
    ring_first = (first_tile - section_index * tiles_dev) % col_blocks
    ring_parts = []
    for k in range(lax.axis_size("section") * tiles_dev):
        start = width + (ring_first + k) * block_size
        piece = lax.dynamic_slice_in_dim(rows_all, start, block_size, 1)
        ring_parts.append(gram(piece))
    ring_parts = jnp.stack(ring_parts)
    own_parts = lax.dynamic_slice_in_dim(ring_parts, section_index * tiles_dev, tiles_dev, 0)
    other_parts = lax.dynamic_slice_in_dim(
        ring_parts, (1 - section_index) * tiles_dev, tiles_dev, 0
    )
    sent = jnp.concatenate([input_part[None], other_parts], axis=0)
    got = lax.ppermute(sent, "section", swap)
    input_pair = input_part + got[0]
    input_sum = input_pair + lax.ppermute(input_pair, "tensor", swap)
    output_sum = own_parts + got[1:]
    input_stats = input_sum[None] / count_input
    output_stats = output_sum * (tokens_all / count_output)
    inverses = invert_blocks(jnp.concatenate([input_stats, output_stats], axis=0))
    left_inverse = inverses[0]
    right_inverse = inverses[1:]

    input_blocks = inputs.reshape(token_rows, row_blocks, block_size)
    grad_blocks = cotangent.reshape(token_rows, col_blocks, block_size)
    all_tiles = jnp.einsum(
        "tir,tjc->ijrc", input_blocks, grad_blocks, preferred_element_type=jnp.float32
    )
    shard_count = lax.axis_size("shard")
    piece_tiles = row_blocks * col_blocks // shard_count
    flat_rows = piece_tiles * block_size * block_size // 128
    all_tiles = all_tiles.reshape(shard_count, flat_rows, 128)
    owned_tiles = lax.psum_scatter(all_tiles, "shard", scatter_dimension=0, tiled=True)
    owned_tiles = owned_tiles.reshape(piece_tiles, block_size, block_size)
    mine = lax.dynamic_slice_in_dim(owned_tiles, section_index * tiles_dev, tiles_dev, 0)
    theirs = lax.dynamic_slice_in_dim(owned_tiles, (1 - section_index) * tiles_dev, tiles_dev, 0)
    grad_tiles = mine + lax.ppermute(theirs, "section", swap)
    left_side = jnp.einsum(
        "rs,ksc->krc", left_inverse, grad_tiles, precision=lax.Precision.HIGHEST
    )
    update = jnp.einsum("krs,ksc->krc", left_side, right_inverse, precision=lax.Precision.HIGHEST)
    velocity_next = momentum_rate * velocity + update[None]
    fresh = (master - learning_rate * velocity_next).astype(jnp.bfloat16)
    fresh_flat = fresh.reshape(1, tiles_dev * block_size * block_size // 128, 128)
    gathered = lax.all_gather(fresh_flat, ("shard", "section"), axis=1, tiled=True)
    weights = (
        gathered.reshape(row_blocks, col_blocks, block_size, block_size)
        .transpose(0, 2, 1, 3)
        .reshape(width, columns)
    )
    return (velocity_next, weights)


def solution(mesh):
    placed = (
        P(("shard", "section"), None),
        P(("shard", "section"), "tensor"),
        P(("shard", "tensor", "section")),
        P("tensor", ("shard", "section"), None, None),
        P("tensor", ("shard", "section"), None, None),
    )
    return jax.shard_map(
        body,
        mesh=mesh,
        in_specs=placed,
        out_specs=(P("tensor", ("shard", "section"), None, None), P(None, "tensor")),
        check_vma=False,
    )
```

```python
import jax
import jax.numpy as jnp
from jax import lax
from jax.sharding import PartitionSpec as P

ITERS = 4
SAMP = 8


damping = 0.1
momentum_rate = 0.9
learning_rate = 0.1


def invert_blocks(stats):
    order = stats.shape[-1]
    identity = jnp.eye(order, dtype=jnp.float32)
    damped = stats + damping * identity
    row_norm = jnp.max(jnp.sum(jnp.abs(damped), axis=2), axis=1)
    approx = identity[None] / row_norm[:, None, None]
    for sweep in range(ITERS):
        product = jnp.einsum("nij,njk->nik", damped, approx, precision=lax.Precision.HIGHEST)
        approx = 2.0 * approx - jnp.einsum(
            "nij,njk->nik", approx, product, precision=lax.Precision.HIGHEST
        )
    return approx


def gram(rows):
    return jnp.einsum("sr,sc->rc", rows, rows, preferred_element_type=jnp.float32)


def body(inputs, cotangent, picks, master, velocity):
    token_rows, width = inputs.shape
    columns = cotangent.shape[1]
    block_size = master.shape[2]
    tiles_dev = master.shape[1]
    row_blocks = width // block_size
    col_blocks = columns // block_size
    count_input = SAMP * lax.axis_size("shard") * lax.axis_size("tensor") * lax.axis_size("section")
    count_output = SAMP * lax.axis_size("shard") * lax.axis_size("section")
    tokens_all = token_rows * lax.axis_size("shard") * lax.axis_size("section")

    first_tile = (
        lax.axis_index("shard") * lax.axis_size("section") + lax.axis_index("section")
    ) * tiles_dev
    positions = first_tile + jnp.arange(tiles_dev, dtype=jnp.int32)
    row_block = first_tile // col_blocks
    col_block_ids = positions % col_blocks

    section_index = lax.axis_index("section")
    swap = [(0, 1), (1, 0)]
    sample_rows = jnp.concatenate(
        [jnp.take(inputs, picks, axis=0), jnp.take(cotangent, picks, axis=0)], axis=1
    )
    rows_all = lax.all_gather(sample_rows, "shard", axis=0, tiled=True)
    input_piece = lax.dynamic_slice_in_dim(rows_all, row_block * block_size, block_size, 1)
    input_part = gram(input_piece)
    ring_first = (first_tile - section_index * tiles_dev) % col_blocks
    ring_parts = []
    for k in range(lax.axis_size("section") * tiles_dev):
        start = width + (ring_first + k) * block_size
        piece = lax.dynamic_slice_in_dim(rows_all, start, block_size, 1)
        ring_parts.append(gram(piece))
    ring_parts = jnp.stack(ring_parts)
    own_parts = lax.dynamic_slice_in_dim(ring_parts, section_index * tiles_dev, tiles_dev, 0)
    other_parts = lax.dynamic_slice_in_dim(
        ring_parts, (1 - section_index) * tiles_dev, tiles_dev, 0
    )
    sent = jnp.concatenate([input_part[None], other_parts], axis=0)
    got = lax.ppermute(sent, "section", swap)
    input_pair = input_part + got[0]
    input_sum = input_pair + lax.ppermute(input_pair, "tensor", swap)
    output_sum = own_parts + got[1:]
    input_stats = input_sum[None] / count_input
    output_stats = output_sum * (tokens_all / count_output)
    inverses = invert_blocks(jnp.concatenate([input_stats, output_stats], axis=0))
    left_inverse = inverses[0]
    right_inverse = inverses[1:]

    shard_count = lax.axis_size("shard")
    shard_index = lax.axis_index("shard")
    group = block_size * shard_count // width
    rows_each = width // shard_count
    chunk = columns // group // 2
    local_grad = jnp.einsum("tr,tc->rc", inputs, cotangent, preferred_element_type=jnp.float32)
    slabs = local_grad.reshape(shard_count, rows_each * columns // 128, 128)
    row_sums = lax.psum_scatter(slabs, "shard", scatter_dimension=0, tiled=True)
    row_sums = row_sums.reshape(rows_each, group, 2, chunk)
    mine = lax.dynamic_index_in_dim(row_sums, section_index, 2, keepdims=False)
    theirs = lax.dynamic_index_in_dim(row_sums, 1 - section_index, 2, keepdims=False)
    half = mine + lax.ppermute(theirs, "section", swap)
    place = shard_index % group
    base = shard_index - place
    arrived = [lax.dynamic_index_in_dim(half, place, 1, keepdims=False)]
    for shift in range(1, group):
        pairs = [
            (src, src - src % group + (src % group + shift) % group) for src in range(shard_count)
        ]
        outgoing = lax.dynamic_index_in_dim(half, (place + shift) % group, 1, keepdims=False)
        arrived.append(lax.ppermute(outgoing, "shard", pairs))
    arrived = jnp.stack(arrived)
    order = (place - jnp.arange(group, dtype=jnp.int32)) % group
    owned_block = jnp.take(arrived, order, axis=0).reshape(block_size, tiles_dev, block_size)
    grad_tiles = owned_block.transpose(1, 0, 2)
    left_side = jnp.einsum(
        "rs,ksc->krc", left_inverse, grad_tiles, precision=lax.Precision.HIGHEST
    )
    update = jnp.einsum("krs,ksc->krc", left_side, right_inverse, precision=lax.Precision.HIGHEST)
    velocity_next = momentum_rate * velocity + update[None]
    fresh = (master - learning_rate * velocity_next).astype(jnp.bfloat16)
    gathered = lax.all_gather(fresh, ("shard", "section"), axis=1, tiled=True)
    weights = (
        gathered.reshape(row_blocks, col_blocks, block_size, block_size)
        .transpose(0, 2, 1, 3)
        .reshape(width, columns)
    )
    return (velocity_next, weights)


def solution(mesh):
    placed = (
        P(("shard", "section"), None),
        P(("shard", "section"), "tensor"),
        P(("shard", "tensor", "section")),
        P("tensor", ("shard", "section"), None, None),
        P("tensor", ("shard", "section"), None, None),
    )
    return jax.shard_map(
        body,
        mesh=mesh,
        in_specs=placed,
        out_specs=(P("tensor", ("shard", "section"), None, None), P(None, "tensor")),
        check_vma=False,
    )
```

```python
import jax
import jax.numpy as jnp
from jax import lax
from jax.sharding import PartitionSpec as P

ITERS = 4
SAMP = 8


damping = 0.1
momentum_rate = 0.9
learning_rate = 0.1


def invert_blocks(stats):
    order = stats.shape[-1]
    identity = jnp.eye(order, dtype=jnp.float32)
    damped = stats + damping * identity
    row_norm = jnp.max(jnp.sum(jnp.abs(damped), axis=2), axis=1)
    approx = identity[None] / row_norm[:, None, None]
    for sweep in range(ITERS):
        product = jnp.einsum("nij,njk->nik", damped, approx, precision=lax.Precision.HIGHEST)
        approx = 2.0 * approx - jnp.einsum(
            "nij,njk->nik", approx, product, precision=lax.Precision.HIGHEST
        )
    return approx


def gram(rows):
    return jnp.einsum("sr,sc->rc", rows, rows, preferred_element_type=jnp.float32)


def body(inputs, cotangent, picks, master, velocity):
    token_rows, width = inputs.shape
    columns = cotangent.shape[1]
    block_size = master.shape[2]
    tiles_dev = master.shape[1]
    row_blocks = width // block_size
    col_blocks = columns // block_size
    count_input = SAMP * lax.axis_size("shard") * lax.axis_size("tensor") * lax.axis_size("section")
    count_output = SAMP * lax.axis_size("shard") * lax.axis_size("section")
    tokens_all = token_rows * lax.axis_size("shard") * lax.axis_size("section")

    first_tile = (
        lax.axis_index("shard") * lax.axis_size("section") + lax.axis_index("section")
    ) * tiles_dev
    positions = first_tile + jnp.arange(tiles_dev, dtype=jnp.int32)
    row_block = first_tile // col_blocks
    col_block_ids = positions % col_blocks

    section_index = lax.axis_index("section")
    swap = [(0, 1), (1, 0)]
    sample_rows = jnp.concatenate(
        [jnp.take(inputs, picks, axis=0), jnp.take(cotangent, picks, axis=0)], axis=1
    )
    rows_all = sample_rows
    distance = 1
    while distance < lax.axis_size("shard"):
        pairs = [(src, src ^ distance) for src in range(lax.axis_size("shard"))]
        rows_all = jnp.concatenate([rows_all, lax.ppermute(rows_all, "shard", pairs)], axis=0)
        distance *= 2
    input_piece = lax.dynamic_slice_in_dim(rows_all, row_block * block_size, block_size, 1)
    input_part = gram(input_piece)
    ring_first = (first_tile - section_index * tiles_dev) % col_blocks
    ring_parts = []
    for k in range(lax.axis_size("section") * tiles_dev):
        start = width + (ring_first + k) * block_size
        piece = lax.dynamic_slice_in_dim(rows_all, start, block_size, 1)
        ring_parts.append(gram(piece))
    ring_parts = jnp.stack(ring_parts)
    own_parts = lax.dynamic_slice_in_dim(ring_parts, section_index * tiles_dev, tiles_dev, 0)
    other_parts = lax.dynamic_slice_in_dim(
        ring_parts, (1 - section_index) * tiles_dev, tiles_dev, 0
    )
    sent = jnp.concatenate([input_part[None], other_parts], axis=0)
    got = lax.ppermute(sent, "section", swap)
    input_pair = input_part + got[0]
    input_sum = input_pair + lax.ppermute(input_pair, "tensor", swap)
    output_sum = own_parts + got[1:]
    input_stats = input_sum[None] / count_input
    output_stats = output_sum * (tokens_all / count_output)
    inverses = invert_blocks(jnp.concatenate([input_stats, output_stats], axis=0))
    left_inverse = inverses[0]
    right_inverse = inverses[1:]

    shard_count = lax.axis_size("shard")
    shard_index = lax.axis_index("shard")
    group = block_size * shard_count // width
    rows_each = width // shard_count
    chunk = columns // group // 2
    local_grad = jnp.einsum("tr,tc->rc", inputs, cotangent, preferred_element_type=jnp.float32)
    slabs = local_grad.reshape(shard_count, rows_each * columns // 128, 128)
    row_sums = lax.psum_scatter(slabs, "shard", scatter_dimension=0, tiled=True)
    row_sums = row_sums.reshape(rows_each, group, 2, chunk)
    mine = lax.dynamic_index_in_dim(row_sums, section_index, 2, keepdims=False)
    theirs = lax.dynamic_index_in_dim(row_sums, 1 - section_index, 2, keepdims=False)
    half = mine + lax.ppermute(theirs, "section", swap)
    place = shard_index % group
    base = shard_index - place
    arrived = [lax.dynamic_index_in_dim(half, place, 1, keepdims=False)]
    for shift in range(1, group):
        pairs = [
            (src, src - src % group + (src % group + shift) % group) for src in range(shard_count)
        ]
        outgoing = lax.dynamic_index_in_dim(half, (place + shift) % group, 1, keepdims=False)
        arrived.append(lax.ppermute(outgoing, "shard", pairs))
    arrived = jnp.stack(arrived)
    order = (place - jnp.arange(group, dtype=jnp.int32)) % group
    owned_block = jnp.take(arrived, order, axis=0).reshape(block_size, tiles_dev, block_size)
    grad_tiles = owned_block.transpose(1, 0, 2)
    left_side = jnp.einsum(
        "rs,ksc->krc", left_inverse, grad_tiles, precision=lax.Precision.HIGHEST
    )
    update = jnp.einsum("krs,ksc->krc", left_side, right_inverse, precision=lax.Precision.HIGHEST)
    velocity_next = momentum_rate * velocity + update[None]
    fresh = (master - learning_rate * velocity_next).astype(jnp.bfloat16)
    gathered = lax.all_gather(fresh, ("shard", "section"), axis=1, tiled=True)
    weights = (
        gathered.reshape(row_blocks, col_blocks, block_size, block_size)
        .transpose(0, 2, 1, 3)
        .reshape(width, columns)
    )
    return (velocity_next, weights)


def solution(mesh):
    placed = (
        P(("shard", "section"), None),
        P(("shard", "section"), "tensor"),
        P(("shard", "tensor", "section")),
        P("tensor", ("shard", "section"), None, None),
        P("tensor", ("shard", "section"), None, None),
    )
    return jax.shard_map(
        body,
        mesh=mesh,
        in_specs=placed,
        out_specs=(P("tensor", ("shard", "section"), None, None), P(None, "tensor")),
        check_vma=False,
    )
```

```python
import jax
import jax.numpy as jnp
from jax import lax
from jax.sharding import PartitionSpec as P
from jax.experimental import pallas as pl

ITERS = 4
SAMP = 8


damping = 0.1
momentum_rate = 0.9
learning_rate = 0.1


def invert_blocks(stats):
    order = stats.shape[-1]
    identity = jnp.eye(order, dtype=jnp.float32)
    damped = stats + damping * identity
    row_norm = jnp.max(jnp.sum(jnp.abs(damped), axis=2), axis=1)
    approx = identity[None] / row_norm[:, None, None]
    for sweep in range(ITERS):
        product = jnp.einsum("nij,njk->nik", damped, approx, precision=lax.Precision.HIGHEST)
        approx = 2.0 * approx - jnp.einsum(
            "nij,njk->nik", approx, product, precision=lax.Precision.HIGHEST
        )
    return approx


def gram(rows):
    return jnp.einsum("sr,sc->rc", rows, rows, preferred_element_type=jnp.float32)


def place_tiles(tiles, row_blocks, col_blocks):
    block_size = tiles.shape[-1]

    def kernel(tile_ref, out_ref):
        for j in range(col_blocks):
            out_ref[:, j * block_size:(j + 1) * block_size] = tile_ref[j]

    size = tiles.size * tiles.dtype.itemsize
    return pl.pallas_call(
        kernel,
        out_shape=jax.ShapeDtypeStruct((row_blocks * block_size, col_blocks * block_size), tiles.dtype),
        grid=(row_blocks,),
        in_specs=[pl.BlockSpec((col_blocks, block_size, block_size), lambda i: (i, 0, 0))],
        out_specs=pl.BlockSpec((block_size, col_blocks * block_size), lambda i: (i, 0)),
        cost_estimate=pl.CostEstimate(flops=0, bytes_accessed=2 * size, transcendentals=0),
    )(tiles)


def body(inputs, cotangent, picks, master, velocity):
    token_rows, width = inputs.shape
    columns = cotangent.shape[1]
    block_size = master.shape[2]
    tiles_dev = master.shape[1]
    row_blocks = width // block_size
    col_blocks = columns // block_size
    count_input = SAMP * lax.axis_size("shard") * lax.axis_size("tensor") * lax.axis_size("section")
    count_output = SAMP * lax.axis_size("shard") * lax.axis_size("section")
    tokens_all = token_rows * lax.axis_size("shard") * lax.axis_size("section")

    first_tile = (
        lax.axis_index("shard") * lax.axis_size("section") + lax.axis_index("section")
    ) * tiles_dev
    positions = first_tile + jnp.arange(tiles_dev, dtype=jnp.int32)
    row_block = first_tile // col_blocks
    col_block_ids = positions % col_blocks

    section_index = lax.axis_index("section")
    swap = [(0, 1), (1, 0)]
    sample_rows = jnp.concatenate(
        [jnp.take(inputs, picks, axis=0), jnp.take(cotangent, picks, axis=0)], axis=1
    )
    rows_all = sample_rows
    distance = 1
    while distance < lax.axis_size("shard"):
        pairs = [(src, src ^ distance) for src in range(lax.axis_size("shard"))]
        rows_all = jnp.concatenate([rows_all, lax.ppermute(rows_all, "shard", pairs)], axis=0)
        distance *= 2
    input_piece = lax.dynamic_slice_in_dim(rows_all, row_block * block_size, block_size, 1)
    input_part = gram(input_piece)
    ring_first = (first_tile - section_index * tiles_dev) % col_blocks
    ring_parts = []
    for k in range(lax.axis_size("section") * tiles_dev):
        start = width + (ring_first + k) * block_size
        piece = lax.dynamic_slice_in_dim(rows_all, start, block_size, 1)
        ring_parts.append(gram(piece))
    ring_parts = jnp.stack(ring_parts)
    own_parts = lax.dynamic_slice_in_dim(ring_parts, section_index * tiles_dev, tiles_dev, 0)
    other_parts = lax.dynamic_slice_in_dim(
        ring_parts, (1 - section_index) * tiles_dev, tiles_dev, 0
    )
    sent = jnp.concatenate([input_part[None], other_parts], axis=0)
    got = lax.ppermute(sent, "section", swap)
    input_pair = input_part + got[0]
    input_sum = input_pair + lax.ppermute(input_pair, "tensor", swap)
    output_sum = own_parts + got[1:]
    input_stats = input_sum[None] / count_input
    output_stats = output_sum * (tokens_all / count_output)
    inverses = invert_blocks(jnp.concatenate([input_stats, output_stats], axis=0))
    left_inverse = inverses[0]
    right_inverse = inverses[1:]

    shard_count = lax.axis_size("shard")
    shard_index = lax.axis_index("shard")
    group = block_size * shard_count // width
    rows_each = width // shard_count
    chunk = columns // group // 2
    local_grad = jnp.einsum("tr,tc->rc", inputs, cotangent, preferred_element_type=jnp.float32)
    slabs = local_grad.reshape(shard_count, rows_each * columns // 128, 128)
    row_sums = lax.psum_scatter(slabs, "shard", scatter_dimension=0, tiled=True)
    row_sums = row_sums.reshape(rows_each, group, 2, chunk)
    mine = lax.dynamic_index_in_dim(row_sums, section_index, 2, keepdims=False)
    theirs = lax.dynamic_index_in_dim(row_sums, 1 - section_index, 2, keepdims=False)
    half = mine + lax.ppermute(theirs, "section", swap)
    place = shard_index % group
    base = shard_index - place
    arrived = [lax.dynamic_index_in_dim(half, place, 1, keepdims=False)]
    for shift in range(1, group):
        pairs = [
            (src, src - src % group + (src % group + shift) % group) for src in range(shard_count)
        ]
        outgoing = lax.dynamic_index_in_dim(half, (place + shift) % group, 1, keepdims=False)
        arrived.append(lax.ppermute(outgoing, "shard", pairs))
    arrived = jnp.stack(arrived)
    order = (place - jnp.arange(group, dtype=jnp.int32)) % group
    owned_block = jnp.take(arrived, order, axis=0).reshape(block_size, tiles_dev, block_size)
    grad_tiles = owned_block.transpose(1, 0, 2)
    left_side = jnp.einsum(
        "rs,ksc->krc", left_inverse, grad_tiles, precision=lax.Precision.HIGHEST
    )
    update = jnp.einsum("krs,ksc->krc", left_side, right_inverse, precision=lax.Precision.HIGHEST)
    velocity_next = momentum_rate * velocity + update[None]
    fresh = (master - learning_rate * velocity_next).astype(jnp.bfloat16)
    gathered = lax.all_gather(fresh, ("shard", "section"), axis=1, tiled=True)
    weights = place_tiles(
        gathered.reshape(row_blocks * col_blocks, block_size, block_size), row_blocks, col_blocks
    )
    return (velocity_next, weights)


def solution(mesh):
    placed = (
        P(("shard", "section"), None),
        P(("shard", "section"), "tensor"),
        P(("shard", "tensor", "section")),
        P("tensor", ("shard", "section"), None, None),
        P("tensor", ("shard", "section"), None, None),
    )
    return jax.shard_map(
        body,
        mesh=mesh,
        in_specs=placed,
        out_specs=(P("tensor", ("shard", "section"), None, None), P(None, "tensor")),
        check_vma=False,
    )
```

```python
import jax
import jax.numpy as jnp
from jax import lax
from jax.sharding import PartitionSpec as P
from jax.experimental import pallas as pl

ITERS = 4
SAMP = 8


damping = 0.1
momentum_rate = 0.9
learning_rate = 0.1


def invert_blocks(stats):
    order = stats.shape[-1]
    identity = jnp.eye(order, dtype=jnp.float32)
    damped = stats + damping * identity
    row_norm = jnp.max(jnp.sum(jnp.abs(damped), axis=2), axis=1)
    approx = identity[None] / row_norm[:, None, None]
    for sweep in range(ITERS):
        product = jnp.einsum("nij,njk->nik", damped, approx, precision=lax.Precision.HIGHEST)
        approx = 2.0 * approx - jnp.einsum(
            "nij,njk->nik", approx, product, precision=lax.Precision.HIGHEST
        )
    return approx


def gram(rows):
    return jnp.einsum("sr,sc->rc", rows, rows, preferred_element_type=jnp.float32)


def place_tiles(tiles, row_blocks, col_blocks):
    block_size = tiles.shape[-1]

    def kernel(tile_ref, out_ref):
        for j in range(col_blocks):
            out_ref[:, j * block_size:(j + 1) * block_size] = tile_ref[j]

    size = tiles.size * tiles.dtype.itemsize
    return pl.pallas_call(
        kernel,
        out_shape=jax.ShapeDtypeStruct((row_blocks * block_size, col_blocks * block_size), tiles.dtype),
        grid=(row_blocks,),
        in_specs=[pl.BlockSpec((col_blocks, block_size, block_size), lambda i: (i, 0, 0))],
        out_specs=pl.BlockSpec((block_size, col_blocks * block_size), lambda i: (i, 0)),
        cost_estimate=pl.CostEstimate(flops=0, bytes_accessed=2 * size, transcendentals=0),
    )(tiles)


def body(inputs, cotangent, picks, master, velocity):
    token_rows, width = inputs.shape
    columns = cotangent.shape[1]
    block_size = master.shape[2]
    tiles_dev = master.shape[1]
    row_blocks = width // block_size
    col_blocks = columns // block_size
    count_input = SAMP * lax.axis_size("shard") * lax.axis_size("tensor") * lax.axis_size("section")
    count_output = SAMP * lax.axis_size("shard") * lax.axis_size("section")
    tokens_all = token_rows * lax.axis_size("shard") * lax.axis_size("section")

    first_tile = (
        lax.axis_index("shard") * lax.axis_size("section") + lax.axis_index("section")
    ) * tiles_dev
    positions = first_tile + jnp.arange(tiles_dev, dtype=jnp.int32)
    row_block = first_tile // col_blocks
    col_block_ids = positions % col_blocks

    section_index = lax.axis_index("section")
    swap = [(0, 1), (1, 0)]
    sample_rows = jnp.concatenate(
        [jnp.take(inputs, picks, axis=0), jnp.take(cotangent, picks, axis=0)], axis=1
    )
    rows_all = sample_rows
    distance = 1
    while distance < lax.axis_size("shard"):
        pairs = [(src, src ^ distance) for src in range(lax.axis_size("shard"))]
        rows_all = jnp.concatenate([rows_all, lax.ppermute(rows_all, "shard", pairs)], axis=0)
        distance *= 2
    input_piece = lax.dynamic_slice_in_dim(rows_all, row_block * block_size, block_size, 1)
    input_part = gram(input_piece)
    ring_first = (first_tile - section_index * tiles_dev) % col_blocks
    ring_parts = []
    for k in range(lax.axis_size("section") * tiles_dev):
        start = width + (ring_first + k) * block_size
        piece = lax.dynamic_slice_in_dim(rows_all, start, block_size, 1)
        ring_parts.append(gram(piece))
    ring_parts = jnp.stack(ring_parts)
    own_parts = lax.dynamic_slice_in_dim(ring_parts, section_index * tiles_dev, tiles_dev, 0)
    other_parts = lax.dynamic_slice_in_dim(
        ring_parts, (1 - section_index) * tiles_dev, tiles_dev, 0
    )
    sent = jnp.concatenate([input_part[None], other_parts], axis=0)
    got = lax.ppermute(sent, "section", swap)
    input_pair = input_part + got[0]
    input_sum = input_pair + lax.ppermute(input_pair, "tensor", swap)
    output_sum = own_parts + got[1:]
    input_stats = input_sum[None] / count_input
    output_stats = output_sum * (tokens_all / count_output)
    inverses = invert_blocks(jnp.concatenate([input_stats, output_stats], axis=0))
    left_inverse = inverses[0]
    right_inverse = inverses[1:]

    shard_count = lax.axis_size("shard")
    shard_index = lax.axis_index("shard")
    group = block_size * shard_count // width
    rows_each = width // shard_count
    chunk = columns // group // 2
    local_grad = jnp.einsum("tr,tc->rc", inputs, cotangent, preferred_element_type=jnp.float32)
    slabs = local_grad.reshape(shard_count, rows_each * columns // 128, 128)
    row_sums = lax.psum_scatter(slabs, "shard", scatter_dimension=0, tiled=True)
    row_sums = row_sums.reshape(rows_each, group, 2, chunk)
    place = shard_index % group
    sections = lax.axis_size("section")
    both = ("shard", "section")
    arrived = []
    for shift in range(group):
        from_sections = []
        for flip in range(sections):
            outgoing = lax.dynamic_index_in_dim(row_sums, (place + shift) % group, 1, keepdims=False)
            outgoing = lax.dynamic_index_in_dim(outgoing, section_index ^ flip, 1, keepdims=False)
            if shift == 0 and flip == 0:
                from_sections.append(outgoing)
                continue
            pairs = []
            for src_shard in range(shard_count):
                for src_section in range(sections):
                    dst_shard = src_shard - src_shard % group + (src_shard % group + shift) % group
                    pairs.append((src_shard * sections + src_section,
                                  dst_shard * sections + (src_section ^ flip)))
            from_sections.append(lax.ppermute(outgoing, both, pairs))
        total = from_sections[0]
        for part in from_sections[1:]:
            total = total + part
        arrived.append(total)
    arrived = jnp.stack(arrived)
    order = (place - jnp.arange(group, dtype=jnp.int32)) % group
    owned_block = jnp.take(arrived, order, axis=0).reshape(block_size, tiles_dev, block_size)
    grad_tiles = owned_block.transpose(1, 0, 2)
    left_side = jnp.einsum(
        "rs,ksc->krc", left_inverse, grad_tiles, precision=lax.Precision.HIGHEST
    )
    update = jnp.einsum("krs,ksc->krc", left_side, right_inverse, precision=lax.Precision.HIGHEST)
    velocity_next = momentum_rate * velocity + update[None]
    fresh = (master - learning_rate * velocity_next).astype(jnp.bfloat16)
    gathered = lax.all_gather(fresh, ("shard", "section"), axis=1, tiled=True)
    weights = place_tiles(
        gathered.reshape(row_blocks * col_blocks, block_size, block_size), row_blocks, col_blocks
    )
    return (velocity_next, weights)


def solution(mesh):
    placed = (
        P(("shard", "section"), None),
        P(("shard", "section"), "tensor"),
        P(("shard", "tensor", "section")),
        P("tensor", ("shard", "section"), None, None),
        P("tensor", ("shard", "section"), None, None),
    )
    return jax.shard_map(
        body,
        mesh=mesh,
        in_specs=placed,
        out_specs=(P("tensor", ("shard", "section"), None, None), P(None, "tensor")),
        check_vma=False,
    )
```

```python
import jax
import jax.numpy as jnp
from jax import lax
from jax.sharding import PartitionSpec as P
from jax.experimental import pallas as pl

ITERS = 4
SAMP = 8


damping = 0.1
momentum_rate = 0.9
learning_rate = 0.1


def invert_blocks(stats):
    order = stats.shape[-1]
    identity = jnp.eye(order, dtype=jnp.float32)
    damped = stats + damping * identity
    row_norm = jnp.max(jnp.sum(jnp.abs(damped), axis=2), axis=1)
    approx = identity[None] / row_norm[:, None, None]
    for sweep in range(ITERS):
        product = jnp.einsum("nij,njk->nik", damped, approx, precision=lax.Precision.HIGHEST)
        approx = 2.0 * approx - jnp.einsum(
            "nij,njk->nik", approx, product, precision=lax.Precision.HIGHEST
        )
    return approx


def gram(rows):
    return jnp.einsum("sr,sc->rc", rows, rows, preferred_element_type=jnp.float32)


def place_tiles(tiles, row_blocks, col_blocks):
    block_size = tiles.shape[-1]

    def kernel(tile_ref, out_ref):
        for j in range(col_blocks):
            out_ref[:, j * block_size:(j + 1) * block_size] = tile_ref[j]

    size = tiles.size * tiles.dtype.itemsize
    return pl.pallas_call(
        kernel,
        out_shape=jax.ShapeDtypeStruct((row_blocks * block_size, col_blocks * block_size), tiles.dtype),
        grid=(row_blocks,),
        in_specs=[pl.BlockSpec((col_blocks, block_size, block_size), lambda i: (i, 0, 0))],
        out_specs=pl.BlockSpec((block_size, col_blocks * block_size), lambda i: (i, 0)),
        cost_estimate=pl.CostEstimate(flops=0, bytes_accessed=2 * size, transcendentals=0),
    )(tiles)


def body(inputs, cotangent, picks, master, velocity):
    token_rows, width = inputs.shape
    columns = cotangent.shape[1]
    block_size = master.shape[2]
    tiles_dev = master.shape[1]
    row_blocks = width // block_size
    col_blocks = columns // block_size
    count_input = SAMP * lax.axis_size("shard") * lax.axis_size("tensor") * lax.axis_size("section")
    count_output = SAMP * lax.axis_size("shard") * lax.axis_size("section")
    tokens_all = token_rows * lax.axis_size("shard") * lax.axis_size("section")

    first_tile = (
        lax.axis_index("shard") * lax.axis_size("section") + lax.axis_index("section")
    ) * tiles_dev
    positions = first_tile + jnp.arange(tiles_dev, dtype=jnp.int32)
    row_block = first_tile // col_blocks
    col_block_ids = positions % col_blocks

    section_index = lax.axis_index("section")
    swap = [(0, 1), (1, 0)]
    sample_rows = jnp.concatenate(
        [jnp.take(inputs, picks, axis=0), jnp.take(cotangent, picks, axis=0)], axis=1
    )
    rows_all = sample_rows
    distance = 1
    while distance < lax.axis_size("shard"):
        pairs = [(src, src ^ distance) for src in range(lax.axis_size("shard"))]
        rows_all = jnp.concatenate([rows_all, lax.ppermute(rows_all, "shard", pairs)], axis=0)
        distance *= 2
    input_piece = lax.dynamic_slice_in_dim(rows_all, row_block * block_size, block_size, 1)
    input_part = gram(input_piece)
    ring_first = (first_tile - section_index * tiles_dev) % col_blocks
    ring_parts = []
    for k in range(lax.axis_size("section") * tiles_dev):
        start = width + (ring_first + k) * block_size
        piece = lax.dynamic_slice_in_dim(rows_all, start, block_size, 1)
        ring_parts.append(gram(piece))
    ring_parts = jnp.stack(ring_parts)
    own_parts = lax.dynamic_slice_in_dim(ring_parts, section_index * tiles_dev, tiles_dev, 0)
    other_parts = lax.dynamic_slice_in_dim(
        ring_parts, (1 - section_index) * tiles_dev, tiles_dev, 0
    )
    sent = jnp.concatenate([input_part[None], other_parts], axis=0)
    got = lax.ppermute(sent, "section", swap)
    input_pair = input_part + got[0]
    input_sum = input_pair + lax.ppermute(input_pair, "tensor", swap)
    output_sum = own_parts + got[1:]
    input_stats = input_sum[None] / count_input
    output_stats = output_sum * (tokens_all / count_output)
    inverses = invert_blocks(jnp.concatenate([input_stats, output_stats], axis=0))
    left_inverse = inverses[0]
    right_inverse = inverses[1:]

    shard_count = lax.axis_size("shard")
    shard_index = lax.axis_index("shard")
    group = block_size * shard_count // width
    rows_each = width // shard_count
    chunk = columns // group // 2
    halves = []
    half_width = columns // 2
    for half in range(2):
        local_grad = jnp.einsum(
            "tr,tc->rc",
            inputs,
            cotangent[:, half * half_width:(half + 1) * half_width],
            preferred_element_type=jnp.float32,
        )
        slabs = local_grad.reshape(shard_count, rows_each * half_width // 128, 128)
        summed = lax.psum_scatter(slabs, "shard", scatter_dimension=0, tiled=True)
        halves.append(summed.reshape(rows_each, half_width))
    row_sums = jnp.concatenate(halves, axis=1).reshape(rows_each, group, 2, chunk)
    mine = lax.dynamic_index_in_dim(row_sums, section_index, 2, keepdims=False)
    theirs = lax.dynamic_index_in_dim(row_sums, 1 - section_index, 2, keepdims=False)
    half = mine + lax.ppermute(theirs, "section", swap)
    place = shard_index % group
    base = shard_index - place
    arrived = [lax.dynamic_index_in_dim(half, place, 1, keepdims=False)]
    for shift in range(1, group):
        pairs = [
            (src, src - src % group + (src % group + shift) % group) for src in range(shard_count)
        ]
        outgoing = lax.dynamic_index_in_dim(half, (place + shift) % group, 1, keepdims=False)
        arrived.append(lax.ppermute(outgoing, "shard", pairs))
    arrived = jnp.stack(arrived)
    order = (place - jnp.arange(group, dtype=jnp.int32)) % group
    owned_block = jnp.take(arrived, order, axis=0).reshape(block_size, tiles_dev, block_size)
    grad_tiles = owned_block.transpose(1, 0, 2)
    left_side = jnp.einsum(
        "rs,ksc->krc", left_inverse, grad_tiles, precision=lax.Precision.HIGHEST
    )
    update = jnp.einsum("krs,ksc->krc", left_side, right_inverse, precision=lax.Precision.HIGHEST)
    velocity_next = momentum_rate * velocity + update[None]
    fresh = (master - learning_rate * velocity_next).astype(jnp.bfloat16)
    gathered = lax.all_gather(fresh, ("shard", "section"), axis=1, tiled=True)
    weights = place_tiles(
        gathered.reshape(row_blocks * col_blocks, block_size, block_size), row_blocks, col_blocks
    )
    return (velocity_next, weights)


def solution(mesh):
    placed = (
        P(("shard", "section"), None),
        P(("shard", "section"), "tensor"),
        P(("shard", "tensor", "section")),
        P("tensor", ("shard", "section"), None, None),
        P("tensor", ("shard", "section"), None, None),
    )
    return jax.shard_map(
        body,
        mesh=mesh,
        in_specs=placed,
        out_specs=(P("tensor", ("shard", "section"), None, None), P(None, "tensor")),
        check_vma=False,
    )
```

```python
import jax
import jax.numpy as jnp
from jax import lax
from jax.sharding import PartitionSpec as P
from jax.experimental import pallas as pl

ITERS = 4
SAMP = 8


damping = 0.1
momentum_rate = 0.9
learning_rate = 0.1


def invert_blocks(stats):
    order = stats.shape[-1]
    identity = jnp.eye(order, dtype=jnp.float32)
    damped = stats + damping * identity
    row_norm = jnp.max(jnp.sum(jnp.abs(damped), axis=2), axis=1)
    approx = identity[None] / row_norm[:, None, None]
    for sweep in range(ITERS):
        product = jnp.einsum("nij,njk->nik", damped, approx, precision=lax.Precision.HIGHEST)
        approx = 2.0 * approx - jnp.einsum(
            "nij,njk->nik", approx, product, precision=lax.Precision.HIGHEST
        )
    return approx


def gram(rows):
    return jnp.einsum("sr,sc->rc", rows, rows, preferred_element_type=jnp.float32)


def place_tiles(tiles, row_blocks, col_blocks):
    block_size = tiles.shape[-1]

    def kernel(tile_ref, out_ref):
        for j in range(col_blocks):
            out_ref[:, j * block_size:(j + 1) * block_size] = tile_ref[j]

    size = tiles.size * tiles.dtype.itemsize
    return pl.pallas_call(
        kernel,
        out_shape=jax.ShapeDtypeStruct((row_blocks * block_size, col_blocks * block_size), tiles.dtype),
        grid=(row_blocks,),
        in_specs=[pl.BlockSpec((col_blocks, block_size, block_size), lambda i: (i, 0, 0))],
        out_specs=pl.BlockSpec((block_size, col_blocks * block_size), lambda i: (i, 0)),
        cost_estimate=pl.CostEstimate(flops=0, bytes_accessed=2 * size, transcendentals=0),
    )(tiles)


def body(inputs, cotangent, picks, master, velocity):
    token_rows, width = inputs.shape
    columns = cotangent.shape[1]
    block_size = master.shape[2]
    tiles_dev = master.shape[1]
    row_blocks = width // block_size
    col_blocks = columns // block_size
    count_input = SAMP * lax.axis_size("shard") * lax.axis_size("tensor") * lax.axis_size("section")
    count_output = SAMP * lax.axis_size("shard") * lax.axis_size("section")
    tokens_all = token_rows * lax.axis_size("shard") * lax.axis_size("section")

    first_tile = (
        lax.axis_index("shard") * lax.axis_size("section") + lax.axis_index("section")
    ) * tiles_dev
    positions = first_tile + jnp.arange(tiles_dev, dtype=jnp.int32)
    row_block = first_tile // col_blocks
    col_block_ids = positions % col_blocks

    section_index = lax.axis_index("section")
    swap = [(0, 1), (1, 0)]
    sample_rows = jnp.concatenate(
        [jnp.take(inputs, picks, axis=0), jnp.take(cotangent, picks, axis=0)], axis=1
    )
    rows_all = sample_rows
    distance = lax.axis_size("shard") // 2
    while distance >= 1:
        pairs = [(src, src ^ distance) for src in range(lax.axis_size("shard"))]
        rows_all = jnp.concatenate([rows_all, lax.ppermute(rows_all, "shard", pairs)], axis=0)
        distance //= 2
    input_piece = lax.dynamic_slice_in_dim(rows_all, row_block * block_size, block_size, 1)
    input_part = gram(input_piece)
    ring_first = (first_tile - section_index * tiles_dev) % col_blocks
    ring_parts = []
    for k in range(lax.axis_size("section") * tiles_dev):
        start = width + (ring_first + k) * block_size
        piece = lax.dynamic_slice_in_dim(rows_all, start, block_size, 1)
        ring_parts.append(gram(piece))
    ring_parts = jnp.stack(ring_parts)
    own_parts = lax.dynamic_slice_in_dim(ring_parts, section_index * tiles_dev, tiles_dev, 0)
    other_parts = lax.dynamic_slice_in_dim(
        ring_parts, (1 - section_index) * tiles_dev, tiles_dev, 0
    )
    sent = jnp.concatenate([input_part[None], other_parts], axis=0)
    got = lax.ppermute(sent, "section", swap)
    input_pair = input_part + got[0]
    input_sum = input_pair + lax.ppermute(input_pair, "tensor", swap)
    output_sum = own_parts + got[1:]
    input_stats = input_sum[None] / count_input
    output_stats = output_sum * (tokens_all / count_output)
    inverses = invert_blocks(jnp.concatenate([input_stats, output_stats], axis=0))
    left_inverse = inverses[0]
    right_inverse = inverses[1:]

    shard_count = lax.axis_size("shard")
    shard_index = lax.axis_index("shard")
    group = block_size * shard_count // width
    rows_each = width // shard_count
    chunk = columns // group // 2
    local_grad = jnp.einsum("tr,tc->rc", inputs, cotangent, preferred_element_type=jnp.float32)
    slabs = local_grad.reshape(shard_count, rows_each * columns // 128, 128)
    row_sums = lax.psum_scatter(slabs, "shard", scatter_dimension=0, tiled=True)
    row_sums = row_sums.reshape(rows_each, group, 2, chunk)
    mine = lax.dynamic_index_in_dim(row_sums, section_index, 2, keepdims=False)
    theirs = lax.dynamic_index_in_dim(row_sums, 1 - section_index, 2, keepdims=False)
    half = mine + lax.ppermute(theirs, "section", swap)
    place = shard_index % group
    base = shard_index - place
    arrived = [lax.dynamic_index_in_dim(half, place, 1, keepdims=False)]
    for shift in range(1, group):
        pairs = [
            (src, src - src % group + (src % group + shift) % group) for src in range(shard_count)
        ]
        outgoing = lax.dynamic_index_in_dim(half, (place + shift) % group, 1, keepdims=False)
        arrived.append(lax.ppermute(outgoing, "shard", pairs))
    arrived = jnp.stack(arrived)
    order = (place - jnp.arange(group, dtype=jnp.int32)) % group
    owned_block = jnp.take(arrived, order, axis=0).reshape(block_size, tiles_dev, block_size)
    grad_tiles = owned_block.transpose(1, 0, 2)
    left_side = jnp.einsum(
        "rs,ksc->krc", left_inverse, grad_tiles, precision=lax.Precision.HIGHEST
    )
    update = jnp.einsum("krs,ksc->krc", left_side, right_inverse, precision=lax.Precision.HIGHEST)
    velocity_next = momentum_rate * velocity + update[None]
    fresh = (master - learning_rate * velocity_next).astype(jnp.bfloat16)
    gathered = lax.all_gather(fresh, ("shard", "section"), axis=1, tiled=True)
    weights = place_tiles(
        gathered.reshape(row_blocks * col_blocks, block_size, block_size), row_blocks, col_blocks
    )
    return (velocity_next, weights)


def solution(mesh):
    placed = (
        P(("shard", "section"), None),
        P(("shard", "section"), "tensor"),
        P(("shard", "tensor", "section")),
        P("tensor", ("shard", "section"), None, None),
        P("tensor", ("shard", "section"), None, None),
    )
    return jax.shard_map(
        body,
        mesh=mesh,
        in_specs=placed,
        out_specs=(P("tensor", ("shard", "section"), None, None), P(None, "tensor")),
        check_vma=False,
    )
```

```python
import jax
import jax.numpy as jnp
from jax import lax
from jax.sharding import PartitionSpec as P
from jax.experimental import pallas as pl

ITERS = 4
SAMP = 8


damping = 0.1
momentum_rate = 0.9
learning_rate = 0.1


def invert_blocks(stats):
    order = stats.shape[-1]
    identity = jnp.eye(order, dtype=jnp.float32)
    damped = stats + damping * identity
    row_norm = jnp.max(jnp.sum(jnp.abs(damped), axis=2), axis=1)
    approx = identity[None] / row_norm[:, None, None]
    for sweep in range(ITERS):
        product = jnp.einsum("nij,njk->nik", damped, approx, precision=lax.Precision.HIGHEST)
        approx = 2.0 * approx - jnp.einsum(
            "nij,njk->nik", approx, product, precision=lax.Precision.HIGHEST
        )
    return approx


def gram(rows):
    return jnp.einsum("sr,sc->rc", rows, rows, preferred_element_type=jnp.float32)


def place_tiles(tiles, row_blocks, col_blocks):
    block_size, piece = tiles.shape[-2], tiles.shape[-1]
    per_row = col_blocks * block_size // piece

    def kernel(tile_ref, out_ref):
        for j in range(per_row):
            out_ref[:, j * piece:(j + 1) * piece] = tile_ref[j]

    size = tiles.size * tiles.dtype.itemsize
    return pl.pallas_call(
        kernel,
        out_shape=jax.ShapeDtypeStruct((row_blocks * block_size, col_blocks * block_size), tiles.dtype),
        grid=(row_blocks,),
        in_specs=[pl.BlockSpec((per_row, block_size, piece), lambda i: (i, 0, 0))],
        out_specs=pl.BlockSpec((block_size, col_blocks * block_size), lambda i: (i, 0)),
        cost_estimate=pl.CostEstimate(flops=0, bytes_accessed=2 * size, transcendentals=0),
    )(tiles)


def body(inputs, cotangent, picks, master, velocity):
    token_rows, width = inputs.shape
    columns = cotangent.shape[1]
    block_size = master.shape[2]
    tiles_dev = master.shape[1]
    row_blocks = width // block_size
    col_blocks = columns // block_size
    count_input = SAMP * lax.axis_size("shard") * lax.axis_size("tensor") * lax.axis_size("section")
    count_output = SAMP * lax.axis_size("shard") * lax.axis_size("section")
    tokens_all = token_rows * lax.axis_size("shard") * lax.axis_size("section")

    first_tile = (
        lax.axis_index("shard") * lax.axis_size("section") + lax.axis_index("section")
    ) * tiles_dev
    positions = first_tile + jnp.arange(tiles_dev, dtype=jnp.int32)
    row_block = first_tile // col_blocks
    col_block_ids = positions % col_blocks

    section_index = lax.axis_index("section")
    swap = [(0, 1), (1, 0)]
    sample_rows = jnp.concatenate(
        [jnp.take(inputs, picks, axis=0), jnp.take(cotangent, picks, axis=0)], axis=1
    )
    rows_all = sample_rows
    distance = lax.axis_size("shard") // 2
    while distance >= 1:
        pairs = [(src, src ^ distance) for src in range(lax.axis_size("shard"))]
        rows_all = jnp.concatenate([rows_all, lax.ppermute(rows_all, "shard", pairs)], axis=0)
        distance //= 2
    input_piece = lax.dynamic_slice_in_dim(rows_all, row_block * block_size, block_size, 1)
    input_part = gram(input_piece)
    ring_first = (first_tile - section_index * tiles_dev) % col_blocks
    ring_parts = []
    for k in range(lax.axis_size("section") * tiles_dev):
        start = width + (ring_first + k) * block_size
        piece = lax.dynamic_slice_in_dim(rows_all, start, block_size, 1)
        ring_parts.append(gram(piece))
    ring_parts = jnp.stack(ring_parts)
    own_parts = lax.dynamic_slice_in_dim(ring_parts, section_index * tiles_dev, tiles_dev, 0)
    other_parts = lax.dynamic_slice_in_dim(
        ring_parts, (1 - section_index) * tiles_dev, tiles_dev, 0
    )
    sent = jnp.concatenate([input_part[None], other_parts], axis=0)
    got = lax.ppermute(sent, "section", swap)
    input_pair = input_part + got[0]
    input_sum = input_pair + lax.ppermute(input_pair, "tensor", swap)
    output_sum = own_parts + got[1:]
    input_stats = input_sum[None] / count_input
    output_stats = output_sum * (tokens_all / count_output)
    inverses = invert_blocks(jnp.concatenate([input_stats, output_stats], axis=0))
    left_inverse = inverses[0]
    right_inverse = inverses[1:]

    shard_count = lax.axis_size("shard")
    shard_index = lax.axis_index("shard")
    group = block_size * shard_count // width
    rows_each = width // shard_count
    chunk = columns // group // 2
    local_grad = jnp.einsum("tr,tc->rc", inputs, cotangent, preferred_element_type=jnp.float32)
    slabs = local_grad.reshape(shard_count, rows_each * columns // 128, 128)
    row_sums = lax.psum_scatter(slabs, "shard", scatter_dimension=0, tiled=True)
    row_sums = row_sums.reshape(rows_each, group, 2, chunk)
    mine = lax.dynamic_index_in_dim(row_sums, section_index, 2, keepdims=False)
    theirs = lax.dynamic_index_in_dim(row_sums, 1 - section_index, 2, keepdims=False)
    half = mine + lax.ppermute(theirs, "section", swap)
    place = shard_index % group
    base = shard_index - place
    arrived = [lax.dynamic_index_in_dim(half, place, 1, keepdims=False)]
    for shift in range(1, group):
        pairs = [
            (src, src - src % group + (src % group + shift) % group) for src in range(shard_count)
        ]
        outgoing = lax.dynamic_index_in_dim(half, (place + shift) % group, 1, keepdims=False)
        arrived.append(lax.ppermute(outgoing, "shard", pairs))
    arrived = jnp.stack(arrived)
    order = (place - jnp.arange(group, dtype=jnp.int32)) % group
    owned_block = jnp.take(arrived, order, axis=0).reshape(block_size, tiles_dev, block_size)
    grad_tiles = owned_block.transpose(1, 0, 2)
    left_side = jnp.einsum(
        "rs,ksc->krc", left_inverse, grad_tiles, precision=lax.Precision.HIGHEST
    )
    update = jnp.einsum("krs,ksc->krc", left_side, right_inverse, precision=lax.Precision.HIGHEST)
    velocity_next = momentum_rate * velocity + update[None]
    fresh = (master - learning_rate * velocity_next).astype(jnp.bfloat16)
    side_by_side = fresh[0].transpose(1, 0, 2).reshape(1, block_size, tiles_dev * block_size)
    gathered = lax.all_gather(side_by_side, ("shard", "section"), axis=0, tiled=True)
    weights = place_tiles(gathered, row_blocks, col_blocks)
    return (velocity_next, weights)


def solution(mesh):
    placed = (
        P(("shard", "section"), None),
        P(("shard", "section"), "tensor"),
        P(("shard", "tensor", "section")),
        P("tensor", ("shard", "section"), None, None),
        P("tensor", ("shard", "section"), None, None),
    )
    return jax.shard_map(
        body,
        mesh=mesh,
        in_specs=placed,
        out_specs=(P("tensor", ("shard", "section"), None, None), P(None, "tensor")),
        check_vma=False,
    )
```

```python
import jax
import jax.numpy as jnp
from jax import lax
from jax.sharding import PartitionSpec as P
from jax.experimental import pallas as pl

ITERS = 4
SAMP = 8


damping = 0.1
momentum_rate = 0.9
learning_rate = 0.1


def invert_blocks(stats):
    order = stats.shape[-1]
    identity = jnp.eye(order, dtype=jnp.float32)
    damped = stats + damping * identity
    row_norm = jnp.max(jnp.sum(jnp.abs(damped), axis=2), axis=1)
    approx = identity[None] / row_norm[:, None, None]
    for sweep in range(ITERS):
        product = jnp.einsum("nij,njk->nik", damped, approx, precision=lax.Precision.HIGHEST)
        approx = 2.0 * approx - jnp.einsum(
            "nij,njk->nik", approx, product, precision=lax.Precision.HIGHEST
        )
    return approx


def gram(rows):
    return jnp.einsum("sr,sc->rc", rows, rows, preferred_element_type=jnp.float32)


def place_tiles(tiles, row_blocks, col_blocks):
    block_size, piece = tiles.shape[-2], tiles.shape[-1]
    per_row = col_blocks * block_size // piece
    slices = 3 if block_size % 48 == 0 else 1
    rows = block_size // slices

    def kernel(tile_ref, out_ref):
        for j in range(per_row):
            out_ref[:, j * piece:(j + 1) * piece] = tile_ref[j]

    size = tiles.size * tiles.dtype.itemsize
    return pl.pallas_call(
        kernel,
        out_shape=jax.ShapeDtypeStruct((row_blocks * block_size, col_blocks * block_size), tiles.dtype),
        grid=(row_blocks, slices),
        in_specs=[pl.BlockSpec((per_row, rows, piece), lambda i, h: (i, h, 0))],
        out_specs=pl.BlockSpec((rows, col_blocks * block_size), lambda i, h: (i * slices + h, 0)),
        cost_estimate=pl.CostEstimate(flops=0, bytes_accessed=2 * size, transcendentals=0),
    )(tiles)


def body(inputs, cotangent, picks, master, velocity):
    token_rows, width = inputs.shape
    columns = cotangent.shape[1]
    block_size = master.shape[2]
    tiles_dev = master.shape[1]
    row_blocks = width // block_size
    col_blocks = columns // block_size
    count_input = SAMP * lax.axis_size("shard") * lax.axis_size("tensor") * lax.axis_size("section")
    count_output = SAMP * lax.axis_size("shard") * lax.axis_size("section")
    tokens_all = token_rows * lax.axis_size("shard") * lax.axis_size("section")

    first_tile = (
        lax.axis_index("shard") * lax.axis_size("section") + lax.axis_index("section")
    ) * tiles_dev
    positions = first_tile + jnp.arange(tiles_dev, dtype=jnp.int32)
    row_block = first_tile // col_blocks
    col_block_ids = positions % col_blocks

    section_index = lax.axis_index("section")
    swap = [(0, 1), (1, 0)]
    sample_rows = jnp.concatenate(
        [jnp.take(inputs, picks, axis=0), jnp.take(cotangent, picks, axis=0)], axis=1
    )
    rows_all = sample_rows
    distance = lax.axis_size("shard") // 2
    while distance >= 1:
        pairs = [(src, src ^ distance) for src in range(lax.axis_size("shard"))]
        rows_all = jnp.concatenate([rows_all, lax.ppermute(rows_all, "shard", pairs)], axis=0)
        distance //= 2
    input_piece = lax.dynamic_slice_in_dim(rows_all, row_block * block_size, block_size, 1)
    input_part = gram(input_piece)
    ring_first = (first_tile - section_index * tiles_dev) % col_blocks
    ring_parts = []
    for k in range(lax.axis_size("section") * tiles_dev):
        start = width + (ring_first + k) * block_size
        piece = lax.dynamic_slice_in_dim(rows_all, start, block_size, 1)
        ring_parts.append(gram(piece))
    ring_parts = jnp.stack(ring_parts)
    own_parts = lax.dynamic_slice_in_dim(ring_parts, section_index * tiles_dev, tiles_dev, 0)
    other_parts = lax.dynamic_slice_in_dim(
        ring_parts, (1 - section_index) * tiles_dev, tiles_dev, 0
    )
    sent = jnp.concatenate([input_part[None], other_parts], axis=0)
    got = lax.ppermute(sent, "section", swap)
    input_pair = input_part + got[0]
    input_sum = input_pair + lax.ppermute(input_pair, "tensor", swap)
    output_sum = own_parts + got[1:]
    input_stats = input_sum[None] / count_input
    output_stats = output_sum * (tokens_all / count_output)
    inverses = invert_blocks(jnp.concatenate([input_stats, output_stats], axis=0))
    left_inverse = inverses[0]
    right_inverse = inverses[1:]

    shard_count = lax.axis_size("shard")
    shard_index = lax.axis_index("shard")
    group = block_size * shard_count // width
    rows_each = width // shard_count
    chunk = columns // group // 2
    local_grad = jnp.einsum("tr,tc->rc", inputs, cotangent, preferred_element_type=jnp.float32)
    slabs = local_grad.reshape(shard_count, rows_each * columns // 128, 128)
    row_sums = lax.psum_scatter(slabs, "shard", scatter_dimension=0, tiled=True)
    row_sums = row_sums.reshape(rows_each, group, 2, chunk)
    mine = lax.dynamic_index_in_dim(row_sums, section_index, 2, keepdims=False)
    theirs = lax.dynamic_index_in_dim(row_sums, 1 - section_index, 2, keepdims=False)
    half = mine + lax.ppermute(theirs, "section", swap)
    place = shard_index % group
    base = shard_index - place
    arrived = [lax.dynamic_index_in_dim(half, place, 1, keepdims=False)]
    for shift in range(1, group):
        pairs = [
            (src, src - src % group + (src % group + shift) % group) for src in range(shard_count)
        ]
        outgoing = lax.dynamic_index_in_dim(half, (place + shift) % group, 1, keepdims=False)
        arrived.append(lax.ppermute(outgoing, "shard", pairs))
    arrived = jnp.stack(arrived)
    order = (place - jnp.arange(group, dtype=jnp.int32)) % group
    owned_block = jnp.take(arrived, order, axis=0).reshape(block_size, tiles_dev, block_size)
    grad_tiles = owned_block.transpose(1, 0, 2)
    left_side = jnp.einsum(
        "rs,ksc->krc", left_inverse, grad_tiles, precision=lax.Precision.HIGHEST
    )
    update = jnp.einsum("krs,ksc->krc", left_side, right_inverse, precision=lax.Precision.HIGHEST)
    velocity_next = momentum_rate * velocity + update[None]
    fresh = (master - learning_rate * velocity_next).astype(jnp.bfloat16)
    side_by_side = fresh[0].transpose(1, 0, 2).reshape(1, block_size, tiles_dev * block_size)
    gathered = lax.all_gather(side_by_side, ("shard", "section"), axis=0, tiled=True)
    weights = place_tiles(gathered, row_blocks, col_blocks)
    return (velocity_next, weights)


def solution(mesh):
    placed = (
        P(("shard", "section"), None),
        P(("shard", "section"), "tensor"),
        P(("shard", "tensor", "section")),
        P("tensor", ("shard", "section"), None, None),
        P("tensor", ("shard", "section"), None, None),
    )
    return jax.shard_map(
        body,
        mesh=mesh,
        in_specs=placed,
        out_specs=(P("tensor", ("shard", "section"), None, None), P(None, "tensor")),
        check_vma=False,
    )
```

```python
import jax
import jax.numpy as jnp
from jax import lax
from jax.sharding import PartitionSpec as P
from jax.experimental import pallas as pl

ITERS = 4
SAMP = 8


damping = 0.1
momentum_rate = 0.9
learning_rate = 0.1


def invert_blocks(stats):
    order = stats.shape[-1]
    identity = jnp.eye(order, dtype=jnp.float32)
    damped = stats + damping * identity
    row_norm = jnp.max(jnp.sum(jnp.abs(damped), axis=2), axis=1)
    approx = identity[None] / row_norm[:, None, None]
    for sweep in range(ITERS):
        product = jnp.einsum("nij,njk->nik", damped, approx, precision=lax.Precision.HIGHEST)
        approx = 2.0 * approx - jnp.einsum(
            "nij,njk->nik", approx, product, precision=lax.Precision.HIGHEST
        )
    return approx


def gram(rows):
    return jnp.einsum("sr,sc->rc", rows, rows, preferred_element_type=jnp.float32)


def place_tiles(tiles, row_blocks, col_blocks):
    block_size, piece = tiles.shape[-2], tiles.shape[-1]
    per_row = col_blocks * block_size // piece

    pair = 2 if row_blocks % 2 == 0 else 1

    def kernel(tile_ref, out_ref):
        for b in range(pair):
            for j in range(per_row):
                out_ref[b * block_size:(b + 1) * block_size, j * piece:(j + 1) * piece] = (
                    tile_ref[b * per_row + j]
                )

    size = tiles.size * tiles.dtype.itemsize
    return pl.pallas_call(
        kernel,
        out_shape=jax.ShapeDtypeStruct((row_blocks * block_size, col_blocks * block_size), tiles.dtype),
        grid=(row_blocks // pair,),
        in_specs=[pl.BlockSpec((pair * per_row, block_size, piece), lambda i: (i, 0, 0))],
        out_specs=pl.BlockSpec((pair * block_size, col_blocks * block_size), lambda i: (i, 0)),
        cost_estimate=pl.CostEstimate(flops=0, bytes_accessed=2 * size, transcendentals=0),
    )(tiles)


def body(inputs, cotangent, picks, master, velocity):
    token_rows, width = inputs.shape
    columns = cotangent.shape[1]
    block_size = master.shape[2]
    tiles_dev = master.shape[1]
    row_blocks = width // block_size
    col_blocks = columns // block_size
    count_input = SAMP * lax.axis_size("shard") * lax.axis_size("tensor") * lax.axis_size("section")
    count_output = SAMP * lax.axis_size("shard") * lax.axis_size("section")
    tokens_all = token_rows * lax.axis_size("shard") * lax.axis_size("section")

    first_tile = (
        lax.axis_index("shard") * lax.axis_size("section") + lax.axis_index("section")
    ) * tiles_dev
    positions = first_tile + jnp.arange(tiles_dev, dtype=jnp.int32)
    row_block = first_tile // col_blocks
    col_block_ids = positions % col_blocks

    section_index = lax.axis_index("section")
    swap = [(0, 1), (1, 0)]
    sample_rows = jnp.concatenate(
        [jnp.take(inputs, picks, axis=0), jnp.take(cotangent, picks, axis=0)], axis=1
    )
    rows_all = sample_rows
    distance = lax.axis_size("shard") // 2
    while distance >= 1:
        pairs = [(src, src ^ distance) for src in range(lax.axis_size("shard"))]
        rows_all = jnp.concatenate([rows_all, lax.ppermute(rows_all, "shard", pairs)], axis=0)
        distance //= 2
    input_piece = lax.dynamic_slice_in_dim(rows_all, row_block * block_size, block_size, 1)
    input_part = gram(input_piece)
    ring_first = (first_tile - section_index * tiles_dev) % col_blocks
    ring_parts = []
    for k in range(lax.axis_size("section") * tiles_dev):
        start = width + (ring_first + k) * block_size
        piece = lax.dynamic_slice_in_dim(rows_all, start, block_size, 1)
        ring_parts.append(gram(piece))
    ring_parts = jnp.stack(ring_parts)
    own_parts = lax.dynamic_slice_in_dim(ring_parts, section_index * tiles_dev, tiles_dev, 0)
    other_parts = lax.dynamic_slice_in_dim(
        ring_parts, (1 - section_index) * tiles_dev, tiles_dev, 0
    )
    sent = jnp.concatenate([input_part[None], other_parts], axis=0)
    got = lax.ppermute(sent, "section", swap)
    input_pair = input_part + got[0]
    input_sum = input_pair + lax.ppermute(input_pair, "tensor", swap)
    output_sum = own_parts + got[1:]
    input_stats = input_sum[None] / count_input
    output_stats = output_sum * (tokens_all / count_output)
    inverses = invert_blocks(jnp.concatenate([input_stats, output_stats], axis=0))
    left_inverse = inverses[0]
    right_inverse = inverses[1:]

    shard_count = lax.axis_size("shard")
    shard_index = lax.axis_index("shard")
    group = block_size * shard_count // width
    rows_each = width // shard_count
    chunk = columns // group // 2
    local_grad = jnp.einsum("tr,tc->rc", inputs, cotangent, preferred_element_type=jnp.float32)
    slabs = local_grad.reshape(shard_count, rows_each * columns // 128, 128)
    row_sums = lax.psum_scatter(slabs, "shard", scatter_dimension=0, tiled=True)
    row_sums = row_sums.reshape(rows_each, group, 2, chunk)
    mine = lax.dynamic_index_in_dim(row_sums, section_index, 2, keepdims=False)
    theirs = lax.dynamic_index_in_dim(row_sums, 1 - section_index, 2, keepdims=False)
    half = mine + lax.ppermute(theirs, "section", swap)
    place = shard_index % group
    base = shard_index - place
    arrived = [lax.dynamic_index_in_dim(half, place, 1, keepdims=False)]
    for shift in range(1, group):
        pairs = [
            (src, src - src % group + (src % group + shift) % group) for src in range(shard_count)
        ]
        outgoing = lax.dynamic_index_in_dim(half, (place + shift) % group, 1, keepdims=False)
        arrived.append(lax.ppermute(outgoing, "shard", pairs))
    arrived = jnp.stack(arrived)
    order = (place - jnp.arange(group, dtype=jnp.int32)) % group
    owned_block = jnp.take(arrived, order, axis=0).reshape(block_size, tiles_dev, block_size)
    grad_tiles = owned_block.transpose(1, 0, 2)
    left_side = jnp.einsum(
        "rs,ksc->krc", left_inverse, grad_tiles, precision=lax.Precision.HIGHEST
    )
    update = jnp.einsum("krs,ksc->krc", left_side, right_inverse, precision=lax.Precision.HIGHEST)
    velocity_next = momentum_rate * velocity + update[None]
    fresh = (master - learning_rate * velocity_next).astype(jnp.bfloat16)
    side_by_side = fresh[0].transpose(1, 0, 2).reshape(1, block_size, tiles_dev * block_size)
    gathered = lax.all_gather(side_by_side, ("shard", "section"), axis=0, tiled=True)
    weights = place_tiles(gathered, row_blocks, col_blocks)
    return (velocity_next, weights)


def solution(mesh):
    placed = (
        P(("shard", "section"), None),
        P(("shard", "section"), "tensor"),
        P(("shard", "tensor", "section")),
        P("tensor", ("shard", "section"), None, None),
        P("tensor", ("shard", "section"), None, None),
    )
    return jax.shard_map(
        body,
        mesh=mesh,
        in_specs=placed,
        out_specs=(P("tensor", ("shard", "section"), None, None), P(None, "tensor")),
        check_vma=False,
    )
```

```python
import jax
import jax.numpy as jnp
from jax import lax
from jax.sharding import PartitionSpec as P
from jax.experimental import pallas as pl

ITERS = 4
SAMP = 8


damping = 0.1
momentum_rate = 0.9
learning_rate = 0.1


def invert_blocks(stats):
    order = stats.shape[-1]
    identity = jnp.eye(order, dtype=jnp.float32)
    damped = stats + damping * identity
    row_norm = jnp.max(jnp.sum(jnp.abs(damped), axis=2), axis=1)
    approx = identity[None] / row_norm[:, None, None]
    for sweep in range(ITERS):
        product = jnp.einsum("nij,njk->nik", damped, approx, precision=lax.Precision.HIGHEST)
        approx = 2.0 * approx - jnp.einsum(
            "nij,njk->nik", approx, product, precision=lax.Precision.HIGHEST
        )
    return approx


def gram(rows):
    return jnp.einsum("sr,sc->rc", rows, rows, preferred_element_type=jnp.float32)


def place_tiles(tiles, row_blocks, col_blocks):
    block_size, piece = tiles.shape[-2], tiles.shape[-1]
    per_row = col_blocks * block_size // piece

    pair = 4 if row_blocks % 4 == 0 else 1

    def kernel(tile_ref, out_ref):
        for b in range(pair):
            for j in range(per_row):
                out_ref[b * block_size:(b + 1) * block_size, j * piece:(j + 1) * piece] = (
                    tile_ref[b * per_row + j]
                )

    size = tiles.size * tiles.dtype.itemsize
    return pl.pallas_call(
        kernel,
        out_shape=jax.ShapeDtypeStruct((row_blocks * block_size, col_blocks * block_size), tiles.dtype),
        grid=(row_blocks // pair,),
        in_specs=[pl.BlockSpec((pair * per_row, block_size, piece), lambda i: (i, 0, 0))],
        out_specs=pl.BlockSpec((pair * block_size, col_blocks * block_size), lambda i: (i, 0)),
        cost_estimate=pl.CostEstimate(flops=0, bytes_accessed=2 * size, transcendentals=0),
    )(tiles)


def body(inputs, cotangent, picks, master, velocity):
    token_rows, width = inputs.shape
    columns = cotangent.shape[1]
    block_size = master.shape[2]
    tiles_dev = master.shape[1]
    row_blocks = width // block_size
    col_blocks = columns // block_size
    count_input = SAMP * lax.axis_size("shard") * lax.axis_size("tensor") * lax.axis_size("section")
    count_output = SAMP * lax.axis_size("shard") * lax.axis_size("section")
    tokens_all = token_rows * lax.axis_size("shard") * lax.axis_size("section")

    first_tile = (
        lax.axis_index("shard") * lax.axis_size("section") + lax.axis_index("section")
    ) * tiles_dev
    positions = first_tile + jnp.arange(tiles_dev, dtype=jnp.int32)
    row_block = first_tile // col_blocks
    col_block_ids = positions % col_blocks

    section_index = lax.axis_index("section")
    swap = [(0, 1), (1, 0)]
    sample_rows = jnp.concatenate(
        [jnp.take(inputs, picks, axis=0), jnp.take(cotangent, picks, axis=0)], axis=1
    )
    rows_all = sample_rows
    distance = lax.axis_size("shard") // 2
    while distance >= 1:
        pairs = [(src, src ^ distance) for src in range(lax.axis_size("shard"))]
        rows_all = jnp.concatenate([rows_all, lax.ppermute(rows_all, "shard", pairs)], axis=0)
        distance //= 2
    input_piece = lax.dynamic_slice_in_dim(rows_all, row_block * block_size, block_size, 1)
    input_part = gram(input_piece)
    ring_first = (first_tile - section_index * tiles_dev) % col_blocks
    ring_parts = []
    for k in range(lax.axis_size("section") * tiles_dev):
        start = width + (ring_first + k) * block_size
        piece = lax.dynamic_slice_in_dim(rows_all, start, block_size, 1)
        ring_parts.append(gram(piece))
    ring_parts = jnp.stack(ring_parts)
    own_parts = lax.dynamic_slice_in_dim(ring_parts, section_index * tiles_dev, tiles_dev, 0)
    other_parts = lax.dynamic_slice_in_dim(
        ring_parts, (1 - section_index) * tiles_dev, tiles_dev, 0
    )
    sent = jnp.concatenate([input_part[None], other_parts], axis=0)
    got = lax.ppermute(sent, "section", swap)
    input_pair = input_part + got[0]
    input_sum = input_pair + lax.ppermute(input_pair, "tensor", swap)
    output_sum = own_parts + got[1:]
    input_stats = input_sum[None] / count_input
    output_stats = output_sum * (tokens_all / count_output)
    inverses = invert_blocks(jnp.concatenate([input_stats, output_stats], axis=0))
    left_inverse = inverses[0]
    right_inverse = inverses[1:]

    shard_count = lax.axis_size("shard")
    shard_index = lax.axis_index("shard")
    group = block_size * shard_count // width
    rows_each = width // shard_count
    chunk = columns // group // 2
    local_grad = jnp.einsum("tr,tc->rc", inputs, cotangent, preferred_element_type=jnp.float32)
    slabs = local_grad.reshape(shard_count, rows_each * columns // 128, 128)
    row_sums = lax.psum_scatter(slabs, "shard", scatter_dimension=0, tiled=True)
    row_sums = row_sums.reshape(rows_each, group, 2, chunk)
    mine = lax.dynamic_index_in_dim(row_sums, section_index, 2, keepdims=False)
    theirs = lax.dynamic_index_in_dim(row_sums, 1 - section_index, 2, keepdims=False)
    half = mine + lax.ppermute(theirs, "section", swap)
    place = shard_index % group
    base = shard_index - place
    arrived = [lax.dynamic_index_in_dim(half, place, 1, keepdims=False)]
    for shift in range(1, group):
        pairs = [
            (src, src - src % group + (src % group + shift) % group) for src in range(shard_count)
        ]
        outgoing = lax.dynamic_index_in_dim(half, (place + shift) % group, 1, keepdims=False)
        arrived.append(lax.ppermute(outgoing, "shard", pairs))
    arrived = jnp.stack(arrived)
    order = (place - jnp.arange(group, dtype=jnp.int32)) % group
    owned_block = jnp.take(arrived, order, axis=0).reshape(block_size, tiles_dev, block_size)
    grad_tiles = owned_block.transpose(1, 0, 2)
    left_side = jnp.einsum(
        "rs,ksc->krc", left_inverse, grad_tiles, precision=lax.Precision.HIGHEST
    )
    update = jnp.einsum("krs,ksc->krc", left_side, right_inverse, precision=lax.Precision.HIGHEST)
    velocity_next = momentum_rate * velocity + update[None]
    fresh = (master - learning_rate * velocity_next).astype(jnp.bfloat16)
    side_by_side = fresh[0].transpose(1, 0, 2).reshape(1, block_size, tiles_dev * block_size)
    gathered = lax.all_gather(side_by_side, ("shard", "section"), axis=0, tiled=True)
    weights = place_tiles(gathered, row_blocks, col_blocks)
    return (velocity_next, weights)


def solution(mesh):
    placed = (
        P(("shard", "section"), None),
        P(("shard", "section"), "tensor"),
        P(("shard", "tensor", "section")),
        P("tensor", ("shard", "section"), None, None),
        P("tensor", ("shard", "section"), None, None),
    )
    return jax.shard_map(
        body,
        mesh=mesh,
        in_specs=placed,
        out_specs=(P("tensor", ("shard", "section"), None, None), P(None, "tensor")),
        check_vma=False,
    )
```
